32 devices in a mesh: groups: 2 (over x), hist: 8 (over z, y), users: 2 (over core).
Axes of the slice: x: 2, y: 2, z: 4, core: 2. Of those that a mesh axis runs over, the one named last changes fastest.
Arguments:
- targets: bfloat16 [4, 512, 1024], P(('groups', 'users'), 'hist'), parts along dimension 0, may hold values from -6 to 6
- hist_keys: bfloat16 [2, 4, 12288, 1024], P(None, ('groups', 'users'), 'hist'), parts along dimension 1, may hold values from -6 to 6
- hist_values: bfloat16 [2, 4, 12288, 1024], P(None, ('groups', 'users'), 'hist'), parts along dimension 1, may hold values from -6 to 6
- lengths: int32 [4], P(('groups', 'users')), parts along dimension 0, may hold values from 3072 to 12288
- cuts: int32 [4, 512], P(('groups', 'users')), parts along dimension 0, may hold values from 1 to 12288
- w_query: bfloat16 [2, 1024, 1024], replicated, may hold values from -0.1875 to 0.1875
- w_gate: bfloat16 [2, 1024, 1024], replicated, may hold values from -0.1875 to 0.1875
- w_out: bfloat16 [2, 1024, 1024], replicated, may hold values from -0.1875 to 0.1875
- ln_gain: float32 [2, 1024], replicated, may hold values from 0.1 to 1.9
Outputs:
- refined: bfloat16 [4, 512, 1024], P(('groups', 'users'), 'hist'), parts along dimension 0
The draws below stay inside these ranges and needn't reach their ends.
There are 2 independent parts, one for each index of `groups`. The reference program is written for one: setup_inputs(seed, part) draws one part's arguments, and reference() takes and returns one part's arrays. A program takes and returns all parts, laid end to end along the dimension named above; an argument that names none is the same for every part. Nothing has to cross between parts.
All inputs are finite; a program needn't handle non-finite values.
Results may differ from the reference program's by a relative error of at most 0.012.
Values may be sent and summed in bfloat16 or wider, within the bound.
A program may use at most 128 MiB of HBM per device.

```python
import math
import jax
import jax.numpy as jnp
from jax import lax

D = 1024
HEADS = 8
LAYERS = 2
TGT = 512
HIST = 12288
USERS = 2


def plant(drawn, stream_key, least, largest):
    spot = [jax.random.randint(jax.random.fold_in(stream_key, axis), (), 0, length) for axis, length in enumerate(drawn.shape)]
    main_axis = drawn.shape.index(max(drawn.shape))
    next_to = spot[:main_axis] + [(spot[main_axis] + 1) % drawn.shape[main_axis]] + spot[main_axis + 1:]
    return drawn.at[tuple(spot)].set(least).at[tuple(next_to)].set(largest)


def block_levels(key, dims, cuts, low, high):
    gain = 1.0
    for position, blocks in cuts:
        steps = jax.random.uniform(jax.random.fold_in(jax.random.fold_in(key, 6), position), (blocks,), jnp.float32, low / len(cuts), high / len(cuts))
        gain = gain * jnp.repeat(jnp.exp(steps), dims[position] // blocks).reshape((-1,) + (1,) * (len(dims) - 1 - position))
    return gain


def gaussian(rng, dims, scale, bound, shards=(), kind=jnp.bfloat16):
    drawn = scale * jax.random.normal(rng, dims, jnp.float32)
    if shards:
        drawn = drawn * block_levels(rng, dims, shards, -0.22, 0.18)
    return jnp.clip(drawn, -bound, bound).astype(kind)


def setup_inputs(seed: int = 0, part: int = 0) -> dict:
    splits = jax.random.split(jax.random.key(seed), 10)
    own_keys = jax.random.split(jax.random.fold_in(splits[9], part), 10)
    return {
        "targets": gaussian(own_keys[0], (USERS, TGT, D), 1.0, 6.0, ((0, 2), (1, 8))),
        "hist_keys": gaussian(own_keys[1], (LAYERS, USERS, HIST, D), 1.0, 6.0, ((1, 2), (2, 8))),
        "hist_values": gaussian(own_keys[2], (LAYERS, USERS, HIST, D), 1.0, 6.0, ((1, 2), (2, 8))),
        "lengths": jax.random.randint(own_keys[3], (USERS,), HIST // 4, HIST + 1).astype(jnp.int32),
        "cuts": plant(jax.random.randint(own_keys[4], (USERS, TGT), 1, HIST + 1), jax.random.fold_in(own_keys[4], 1), 1, HIST).astype(jnp.int32),
        "w_query": gaussian(splits[5], (LAYERS, D, D), D ** -0.5, 0.1875),
        "w_gate": gaussian(splits[6], (LAYERS, D, D), D ** -0.5, 0.1875),
        "w_out": gaussian(splits[7], (LAYERS, D, D), D ** -0.5, 0.1875),
        "ln_gain": jnp.clip(1.0 + 0.18 * jax.random.normal(splits[8], (LAYERS, D), jnp.float32), 0.1, 1.9),
    }


def attend(queries, key_slab, value_slab, limits):
    head_size = D // HEADS
    factor = 1.0 / math.sqrt(head_size)
    positions = jnp.arange(HIST, dtype=jnp.int32)
    visible = positions[None, :] < limits[:, None]
    query_heads = queries.reshape(TGT, HEADS, head_size).transpose(1, 0, 2)
    key_heads = key_slab.reshape(HIST, HEADS, head_size).transpose(1, 0, 2)
    value_heads = value_slab.reshape(HIST, HEADS, head_size).transpose(1, 0, 2)

    def one_head(operands):
        query_head, key_head, value_head = operands
        scores = jnp.dot(query_head, key_head.T, preferred_element_type=jnp.float32) * factor
        weights = jnp.where(visible, jax.nn.silu(scores), 0.0).astype(jnp.bfloat16)
        return jnp.dot(weights, value_head, preferred_element_type=jnp.float32)
    outputs = lax.map(one_head, (query_heads, key_heads, value_heads))
    return outputs.transpose(1, 0, 2).reshape(TGT, D)

def finish(hidden, summed, gating, out_weight, gain_row):
    centre = lax.optimization_barrier(jnp.mean(summed, axis=-1, keepdims=True))
    spread = lax.optimization_barrier(jnp.mean(jnp.square(summed - centre), axis=-1, keepdims=True))
    normed = ((summed - centre) * lax.rsqrt(spread + 1e-05) * gain_row * gating).astype(jnp.bfloat16)
    update = jnp.dot(normed, out_weight, preferred_element_type=jnp.float32)
    return (hidden.astype(jnp.float32) + update).astype(jnp.bfloat16)

def reference(targets, hist_keys, hist_values, lengths, cuts, w_query, w_gate, w_out, ln_gain):
    results = []
    for member in range(USERS):
        hidden = targets[member]
        limits = jnp.minimum(cuts[member], lengths[member])
        for layer_index in range(LAYERS):
            queries = jax.nn.silu(jnp.dot(hidden, w_query[layer_index], preferred_element_type=jnp.float32)).astype(jnp.bfloat16)
            gating = jax.nn.silu(jnp.dot(hidden, w_gate[layer_index], preferred_element_type=jnp.float32))
            summed = attend(queries, hist_keys[layer_index, member], hist_values[layer_index, member], limits)
            hidden = finish(hidden, summed, gating, w_out[layer_index], ln_gain[layer_index])
        results.append(hidden)
    return jnp.stack(results)
```

```python
import functools
import math

import jax
import jax.numpy as jnp
from jax import lax
from jax.experimental import pallas as pl
from jax.experimental.pallas import tpu as pltpu
from jax.sharding import PartitionSpec as P

HEADS = 8
MESH = pl.DeviceIdType.MESH


def half_silu(t):
    return t + t * jnp.tanh(t)


def tile_of(size, most):
    while size % most:
        most //= 2
    return most


def kernel(
    ny, nz, lim_ref, tgt_ref, keys_ref, vals_ref, wq_ref, wg_ref, wo_ref, gain_ref, out_ref,
    kbuf, vbuf, wqb, wgb, wob, q_all, pair, s1, r1, s2, r2, gate, hid, proj, normed,
    in_sem, zs_sem, zr_sem, fs_sem, fr_sem, s1_sem, r1_sem, s2_sem, r2_sem,
):
    me = lax.axis_index("hist")
    z, y = me // ny, me % ny
    layers, hist, width = kbuf.shape
    rows = tgt_ref.shape[0]
    head = width // HEADS
    factor = 0.5 / math.sqrt(head)
    wide = tile_of(width, 256)
    chunk = tile_of(hist, 256)

    def at(zz, yy):
        return {"hist": zz * ny + yy}

    loads = []
    for l in range(layers):
        for k, (src, dst) in enumerate(
            ((wq_ref, wqb), (keys_ref, kbuf), (vals_ref, vbuf), (wg_ref, wgb), (wo_ref, wob))
        ):
            copy = pltpu.make_async_copy(src.at[l], dst.at[l], in_sem.at[l, k])
            copy.start()
            loads.append(copy)

    barrier = pltpu.get_barrier_semaphore()
    for j in range(1, nz):
        pl.semaphore_signal(barrier, inc=1, device_id=at((z + j) % nz, y), device_id_type=MESH)
    if ny == 2:
        pl.semaphore_signal(barrier, inc=1, device_id=at(z, 1 - y), device_id_type=MESH)
    hid[...] = tgt_ref[...]

    def project(w_ref, store):
        def body(i, carry):
            cols = pl.ds(pl.multiple_of(i * wide, wide), wide)
            v = jnp.dot(hid[...], w_ref[:, cols], preferred_element_type=jnp.float32)
            store(cols, half_silu(v * 0.5))
            return carry

        lax.fori_loop(0, width // wide, body, 0)

    sends = []

    def send(src, dst, ss, rs, dev):
        copy = pltpu.make_async_remote_copy(
            src_ref=src, dst_ref=dst, send_sem=ss, recv_sem=rs, device_id=dev, device_id_type=MESH
        )
        copy.start()
        sends.append(copy)
        return copy

    for l in range(layers):
        base = l * 5
        loads[base].wait()

        def put_q(cols, v):
            q_all[l, z, y, :, cols] = v.astype(jnp.bfloat16)

        project(wqb.at[l], put_q)
        if l == 0:
            pl.semaphore_wait(barrier, nz - 1 + ny - 1)

        mine = q_all.at[l, z, y]
        fy = [None] * nz
        zc = [None] * nz
        if ny == 2:
            fy[0] = send(mine, mine, fs_sem.at[l, 0], fr_sem.at[l, 0], at(z, 1 - y))
        for j in range(1, nz):
            zc[j] = send(mine, mine, zs_sem.at[l, j], zr_sem.at[l, j], at((z + j) % nz, y))

        loads[base + 3].wait()

        def put_gate(cols, v):
            gate[:, cols] = v

        project(wgb.at[l], put_gate)
        loads[base + 1].wait()
        loads[base + 2].wait()
        c1 = [None] * nz
        c2 = [None] * nz

        def attend(j):
            zj = (z - j + nz) % nz
            limit = lim_ref[pl.ds(pl.multiple_of(zj * ny * rows, ny * rows), ny * rows), :]

            def body(h, carry):
                cols = pl.ds(pl.multiple_of(h * head, head), head)
                q = q_all[l, zj, :, :, cols].reshape(ny * rows, head)
                total = jnp.zeros((ny * rows, head), jnp.float32)
                for c in range(0, hist, chunk):
                    s = lax.dot_general(
                        q, kbuf[l, c : c + chunk, cols], (((1,), (1,)), ((), ())),
                        preferred_element_type=jnp.float32,
                    )
                    w = half_silu(s * factor)
                    pos = lax.broadcasted_iota(jnp.int32, s.shape, 1) + c
                    w = jnp.where(pos < limit, w, 0.0).astype(jnp.bfloat16)
                    total += jnp.dot(
                        w, vbuf[l, c : c + chunk, cols], preferred_element_type=jnp.float32
                    )
                pair[j, :, :, cols] = total.reshape(ny, rows, head)
                return carry

            lax.fori_loop(0, HEADS, body, 0)

        def reduce(j):
            if j == 0:
                return
            term = pair[j, y]
            if ny == 2:
                c1[j].wait_recv()
                term = term + r1[l, j].astype(jnp.float32)
            s2[l, j] = term.astype(jnp.bfloat16)
            c2[j] = send(
                s2.at[l, j], r2.at[l, j], s2_sem.at[l, j], r2_sem.at[l, j],
                at((z - j + nz) % nz, y),
            )

        for j in range(nz):
            if j + 1 < nz:
                zc[j + 1].wait_recv()
                if ny == 2:
                    block = q_all.at[l, (z - j - 1 + nz) % nz, y]
                    fy[j + 1] = send(
                        block, block, fs_sem.at[l, j + 1], fr_sem.at[l, j + 1], at(z, 1 - y)
                    )
            if ny == 2:
                fy[j].wait_recv()
            attend(j)
            if ny == 2:
                s1[l, j] = pair[j, 1 - y].astype(jnp.bfloat16)
                c1[j] = send(
                    s1.at[l, j], r1.at[l, j], s1_sem.at[l, j], r1_sem.at[l, j], at(z, 1 - y)
                )
            if j > 0:
                reduce(j - 1)
        reduce(nz - 1)

        summed = pair[0, y]
        if ny == 2:
            c1[0].wait_recv()
            summed = summed + r1[l, 0].astype(jnp.float32)
        for j in range(1, nz):
            c2[j].wait_recv()
            summed = summed + r2[l, j].astype(jnp.float32)
        centre = jnp.mean(summed, axis=-1, keepdims=True)
        summed = summed - centre
        spread = jnp.mean(jnp.square(summed), axis=-1, keepdims=True)
        normed[...] = (
            summed * lax.rsqrt(spread + 1e-05) * gain_ref[l : l + 1, :] * gate[...]
        ).astype(jnp.bfloat16)
        loads[base + 4].wait()
        target = out_ref if l == layers - 1 else proj

        def out_body(i, carry):
            cols = pl.ds(pl.multiple_of(i * wide, wide), wide)
            update = jnp.dot(normed[...], wob[l, :, cols], preferred_element_type=jnp.float32)
            target[:, cols] = (hid[:, cols].astype(jnp.float32) + update).astype(jnp.bfloat16)
            return carry

        lax.fori_loop(0, width // wide, out_body, 0)
        if l < layers - 1:
            hid[...] = proj[...]

    for copy in sends:
        copy.wait_send()


def inner_size(mesh):
    try:
        spot = mesh.axis_names.index("hist")
        line = mesh.devices.transpose(
            [spot] + [a for a in range(mesh.devices.ndim) if a != spot]
        ).reshape(mesh.devices.shape[spot], -1)[:, 0]
        ys = len({d.coords[1] for d in line})
    except (AttributeError, ValueError):
        ys = 1
    return ys if ys in (1, 2) and len(line) % ys == 0 else 1


def per_device(
    ny, targets, hist_keys, hist_values, lengths, cuts, w_query, w_gate, w_out, ln_gain
):
    layers, _, hist, width = hist_keys.shape
    rows = targets.shape[1]
    n = lax.axis_size("hist")
    nz = n // ny
    offset = lax.axis_index("hist") * hist
    limits = (jnp.minimum(cuts[0], lengths[0]) - offset)[:, None]
    bf, f32 = jnp.bfloat16, jnp.float32
    vmem = pl.BlockSpec(memory_space=pltpu.VMEM)
    hbm = pl.BlockSpec(memory_space=pl.ANY)
    dma = pltpu.SemaphoreType.DMA
    refined = pl.pallas_call(
        functools.partial(kernel, ny, nz),
        out_shape=jax.ShapeDtypeStruct((rows, width), bf),
        in_specs=[vmem, vmem, hbm, hbm, hbm, hbm, hbm, vmem],
        out_specs=vmem,
        scratch_shapes=[
            pltpu.VMEM((layers, hist, width), bf),
            pltpu.VMEM((layers, hist, width), bf),
            pltpu.VMEM((layers, width, width), bf),
            pltpu.VMEM((layers, width, width), bf),
            pltpu.VMEM((layers, width, width), bf),
            pltpu.VMEM((layers, nz, ny, rows, width), bf),
            pltpu.VMEM((nz, ny, rows, width), f32),
            pltpu.VMEM((layers, nz, rows, width), bf),
            pltpu.VMEM((layers, nz, rows, width), bf),
            pltpu.VMEM((layers, nz, rows, width), bf),
            pltpu.VMEM((layers, nz, rows, width), bf),
            pltpu.VMEM((rows, width), f32),
            pltpu.VMEM((rows, width), bf),
            pltpu.VMEM((rows, width), bf),
            pltpu.VMEM((rows, width), bf),
            dma((layers, 5)),
        ]
        + [dma((layers, nz))] * 8,
        compiler_params=pltpu.CompilerParams(
            collective_id=0, has_side_effects=True, vmem_limit_bytes=60 * 2**20
        ),
    )(
        limits, targets[0], hist_keys[:, 0], hist_values[:, 0], w_query, w_gate, w_out, ln_gain
    )
    return refined[None]


def solution(mesh):
    return jax.shard_map(
        functools.partial(per_device, inner_size(mesh)),
        mesh=mesh,
        in_specs=(
            P(("groups", "users"), "hist", None),
            P(None, ("groups", "users"), "hist", None),
            P(None, ("groups", "users"), "hist", None),
            P(("groups", "users")),
            P(("groups", "users"), None),
            P(),
            P(),
            P(),
            P(),
        ),
        out_specs=P(("groups", "users"), "hist", None),
        check_vma=False,
    )
```

```python
import functools
import math

import jax
import jax.numpy as jnp
from jax import lax
from jax.experimental import pallas as pl
from jax.experimental.pallas import tpu as pltpu
from jax.sharding import PartitionSpec as P

HEADS = 8
GROUPS = 2
PARTS = 2
CHUNK = 256
UNROLL = 2
MESH = pl.DeviceIdType.MESH


def half_silu(t):
    return t + t * jnp.tanh(t)


def tile_of(size, most):
    while size % most:
        most //= 2
    return most


def kernel(
    ny, nz, lim_ref, tgt_ref, keys_ref, vals_ref, wq_ref, wg_ref, wo_ref, gain_ref, out_ref,
    kbuf, vbuf, wqb, wgb, wob, q_all, res, s1, r1, s2, r2, gate, hid, normed,
    in_sem, zs_sem, zr_sem, fs_sem, fr_sem, s1_sem, r1_sem, s2_sem, r2_sem,
):
    me = lax.axis_index("hist")
    z, y = me // ny, me % ny
    layers, hist, width = kbuf.shape
    parts = s1.shape[2]
    rows = tgt_ref.shape[0] // GROUPS
    head = width // HEADS
    factor = 0.5 / math.sqrt(head)
    wide = tile_of(width, 256)
    chunk = tile_of(hist, CHUNK)
    span = width // parts
    total_rows = nz * ny * rows
    bf, f32 = jnp.bfloat16, jnp.float32

    def at(zz, yy):
        return {"hist": zz * ny + yy}

    loads = []
    for l in range(layers):
        for k, (src, dst) in enumerate(
            ((wq_ref, wqb), (keys_ref, kbuf), (vals_ref, vbuf), (wg_ref, wgb), (wo_ref, wob))
        ):
            copy = pltpu.make_async_copy(src.at[l], dst.at[l], in_sem.at[l, k])
            copy.start()
            loads.append(copy)

    barrier = pltpu.get_barrier_semaphore()
    for j in range(1, nz):
        pl.semaphore_signal(barrier, inc=1, device_id=at((z + j) % nz, y), device_id_type=MESH)
    if ny == 2:
        pl.semaphore_signal(barrier, inc=1, device_id=at(z, 1 - y), device_id_type=MESH)
    hid[...] = tgt_ref[...].reshape(hid.shape)

    copies = {}

    def send(name, src, dst, ss, rs, dev):
        copy = pltpu.make_async_remote_copy(
            src_ref=src, dst_ref=dst, send_sem=ss, recv_sem=rs, device_id=dev, device_id_type=MESH
        )
        copy.start()
        copies[name] = copy

    def columns(i, size):
        return pl.ds(pl.multiple_of(i * size, size), size)

    def project(w_ref, g0, g1, store):
        def body(i, carry):
            cols = columns(i, wide)
            x = hid[g0:g1].reshape((g1 - g0) * rows, width)
            v = jnp.dot(x, w_ref[:, cols], preferred_element_type=f32)
            v = half_silu(v * 0.5)
            for g in range(g0, g1):
                store(g, cols, v[(g - g0) * rows : (g - g0 + 1) * rows])
            return carry

        lax.fori_loop(0, width // wide, body, 0, unroll=2)

    def query(l, g0, g1):
        def store(g, cols, v):
            q_all[l, g, z, y, :, cols] = v.astype(bf)

        project(wqb.at[l], g0, g1, store)

    def spread(l, g):
        mine = q_all.at[l, g, z, y]
        if ny == 2:
            send(("f", l, g, 0), mine, mine, fs_sem.at[l, g, 0], fr_sem.at[l, g, 0], at(z, 1 - y))
        for j in range(1, nz):
            send(
                ("z", l, g, j), mine, mine, zs_sem.at[l, g, j], zr_sem.at[l, g, j],
                at((z + j) % nz, y),
            )

    def gating(l, g0, g1):
        def store(g, cols, v):
            gate[g, :, cols] = v

        project(wgb.at[l], g0, g1, store)

    def forward(l, g):
        for j in range(1, nz):
            copies["z", l, g, j].wait_recv()
            if ny == 2:
                block = q_all.at[l, g, (z - j + nz) % nz, y]
                send(
                    ("f", l, g, j), block, block, fs_sem.at[l, g, j], fr_sem.at[l, g, j],
                    at(z, 1 - y),
                )

    def arrive(l, g):
        if ny == 2:
            for j in range(nz):
                copies["f", l, g, j].wait_recv()

    def attend(l, g, p):
        def body(i, carry):
            cols = columns(p * (HEADS // parts) + i, head)
            q = q_all[l, g, :, :, :, cols].reshape(total_rows, head)
            limit = lim_ref[g]
            total = jnp.zeros((total_rows, head), f32)
            for c in range(0, hist, chunk):
                s = lax.dot_general(
                    q, kbuf[l, c : c + chunk, cols], (((1,), (1,)), ((), ())),
                    preferred_element_type=f32,
                )
                w = half_silu((s * factor).astype(bf))
                pos = lax.broadcasted_iota(jnp.int32, s.shape, 1) + c
                w = jnp.where(pos < limit, w, jnp.bfloat16(0.0))
                total += jnp.dot(w, vbuf[l, c : c + chunk, cols], preferred_element_type=f32)
            res[g, :, :, :, cols] = total.reshape(nz, ny, rows, head)
            return carry

        lax.fori_loop(0, HEADS // parts, body, 0, unroll=UNROLL)
        if ny == 2:
            s1[l, g, p] = res[g, :, 1 - y, :, p * span : (p + 1) * span].astype(bf)
            send(
                ("1", l, g, p), s1.at[l, g, p], r1.at[l, g, p], s1_sem.at[l, g, p],
                r1_sem.at[l, g, p], at(z, 1 - y),
            )

    def reduce(l, g, p):
        if ny == 2:
            copies["1", l, g, p].wait_recv()
        for j in range(1, nz):
            zj = (z - j + nz) % nz
            term = res[g, zj, y, :, p * span : (p + 1) * span]
            if ny == 2:
                term = term + r1[l, g, p, zj].astype(f32)
            s2[l, g, p, j] = term.astype(bf)
            send(
                ("2", l, g, p, j), s2.at[l, g, p, j], r2.at[l, g, p, j], s2_sem.at[l, g, p, j],
                r2_sem.at[l, g, p, j], at(zj, y),
            )

    def finish(l, g):
        sums = []
        for p in range(parts):
            term = res[g, z, y, :, p * span : (p + 1) * span]
            if ny == 2:
                term = term + r1[l, g, p, z].astype(f32)
            for j in range(1, nz):
                copies["2", l, g, p, j].wait_recv()
                term = term + r2[l, g, p, j].astype(f32)
            sums.append(term)
        centre = sum(jnp.sum(t, axis=-1, keepdims=True) for t in sums) / width
        sums = [t - centre for t in sums]
        variance = sum(jnp.sum(jnp.square(t), axis=-1, keepdims=True) for t in sums) / width
        scale = lax.rsqrt(variance + 1e-05)
        for p, t in enumerate(sums):
            cols = slice(p * span, (p + 1) * span)
            normed[g, :, cols] = (t * scale * gain_ref[l : l + 1, cols] * gate[g, :, cols]).astype(bf)

        def body(i, carry):
            cols = columns(i, wide)
            update = jnp.dot(normed[g], wob[l, :, cols], preferred_element_type=f32)
            new = (hid[g, :, cols].astype(f32) + update).astype(bf)
            if l == layers - 1:
                out_ref[g * rows : (g + 1) * rows, cols] = new
            else:
                hid[g, :, cols] = new
            return carry

        lax.fori_loop(0, width // wide, body, 0, unroll=2)

    for l in range(layers):
        wait = loads[l * 5 : l * 5 + 5]
        if l == 0:
            wait[0].wait()
            query(0, 0, GROUPS)
            pl.semaphore_wait(barrier, nz - 1 + ny - 1)
            for g in range(GROUPS):
                spread(0, g)
            wait[3].wait()
            gating(0, 0, GROUPS)
        else:
            prev = GROUPS - 1
            wait[0].wait()
            for g in range(GROUPS):
                if g == prev:
                    reduce(l - 1, prev, parts - 1)
                finish(l - 1, g)
                query(l, g, g + 1)
                spread(l, g)
            wait[3].wait()
            gating(l, 0, GROUPS)
        wait[1].wait()
        wait[2].wait()
        wait[4].wait()
        forward(l, 0)
        arrive(l, 0)
        for g in range(GROUPS):
            for p in range(parts):
                attend(l, g, p)
                if p == 0 and g + 1 < GROUPS:
                    forward(l, g + 1)
                if p > 0:
                    reduce(l, g, p - 1)
                elif g > 0:
                    reduce(l, g - 1, parts - 1)
            if g + 1 < GROUPS:
                arrive(l, g + 1)
    last = layers - 1
    for g in range(GROUPS):
        if g == GROUPS - 1:
            reduce(last, g, parts - 1)
        finish(last, g)

    for copy in copies.values():
        copy.wait_send()


def inner_size(mesh):
    try:
        spot = mesh.axis_names.index("hist")
        line = mesh.devices.transpose(
            [spot] + [a for a in range(mesh.devices.ndim) if a != spot]
        ).reshape(mesh.devices.shape[spot], -1)[:, 0]
        ys = len({d.coords[1] for d in line})
    except (AttributeError, ValueError):
        ys = 1
    return ys if ys in (1, 2) and len(line) % ys == 0 else 1


def per_device(
    ny, targets, hist_keys, hist_values, lengths, cuts, w_query, w_gate, w_out, ln_gain
):
    layers, _, hist, width = hist_keys.shape
    rows = targets.shape[1]
    n = lax.axis_size("hist")
    nz = n // ny
    offset = lax.axis_index("hist") * hist
    rows //= GROUPS
    limits = jnp.minimum(cuts[0], lengths[0]) - offset
    limits = limits.reshape(n, GROUPS, rows).transpose(1, 0, 2).reshape(GROUPS, n * rows, 1)
    bf, f32 = jnp.bfloat16, jnp.float32
    vmem = pl.BlockSpec(memory_space=pltpu.VMEM)
    hbm = pl.BlockSpec(memory_space=pl.ANY)
    dma = pltpu.SemaphoreType.DMA
    span = width // PARTS
    refined = pl.pallas_call(
        functools.partial(kernel, ny, nz),
        out_shape=jax.ShapeDtypeStruct((GROUPS * rows, width), bf),
        in_specs=[vmem, vmem, hbm, hbm, hbm, hbm, hbm, vmem],
        out_specs=vmem,
        scratch_shapes=[
            pltpu.VMEM((layers, hist, width), bf),
            pltpu.VMEM((layers, hist, width), bf),
            pltpu.VMEM((layers, width, width), bf),
            pltpu.VMEM((layers, width, width), bf),
            pltpu.VMEM((layers, width, width), bf),
            pltpu.VMEM((layers, GROUPS, nz, ny, rows, width), bf),
            pltpu.VMEM((GROUPS, nz, ny, rows, width), f32),
            pltpu.VMEM((layers, GROUPS, PARTS, nz, rows, span), bf),
            pltpu.VMEM((layers, GROUPS, PARTS, nz, rows, span), bf),
            pltpu.VMEM((layers, GROUPS, PARTS, nz, rows, span), bf),
            pltpu.VMEM((layers, GROUPS, PARTS, nz, rows, span), bf),
            pltpu.VMEM((GROUPS, rows, width), f32),
            pltpu.VMEM((GROUPS, rows, width), bf),
            pltpu.VMEM((GROUPS, rows, width), bf),
            dma((layers, 5)),
        ]
        + [dma((layers, GROUPS, nz))] * 4
        + [dma((layers, GROUPS, PARTS))] * 2
        + [dma((layers, GROUPS, PARTS, nz))] * 2,
        compiler_params=pltpu.CompilerParams(
            collective_id=0, has_side_effects=True, vmem_limit_bytes=60 * 2**20
        ),
    )(
        limits, targets[0], hist_keys[:, 0], hist_values[:, 0], w_query, w_gate, w_out, ln_gain
    )
    return refined[None]


def solution(mesh):
    return jax.shard_map(
        functools.partial(per_device, inner_size(mesh)),
        mesh=mesh,
        in_specs=(
            P(("groups", "users"), "hist", None),
            P(None, ("groups", "users"), "hist", None),
            P(None, ("groups", "users"), "hist", None),
            P(("groups", "users")),
            P(("groups", "users"), None),
            P(),
            P(),
            P(),
            P(),
        ),
        out_specs=P(("groups", "users"), "hist", None),
        check_vma=False,
    )
```

```python
import functools
import math

import jax
import jax.numpy as jnp
from jax import lax
from jax.experimental import pallas as pl
from jax.experimental.pallas import tpu as pltpu
from jax.sharding import PartitionSpec as P

HEADS = 8
GROUPS = 2
PARTS = 2
CHUNK = 256
UNROLL = 4
MESH = pl.DeviceIdType.MESH


def half_silu(t):
    return t + t * jnp.tanh(t)


def tile_of(size, most):
    while size % most:
        most //= 2
    return most


def kernel(
    ny, nz, lim_ref, tgt_ref, keys_ref, vals_ref, wq_ref, wg_ref, wo_ref, gain_ref, out_ref,
    kbuf, vbuf, wqb, wgb, wob, q_all, res, s1, r1, s2, r2, gate, hid, normed,
    in_sem, zs_sem, zr_sem, fs_sem, fr_sem, s1_sem, r1_sem, s2_sem, r2_sem,
):
    me = lax.axis_index("hist")
    z, y = me // ny, me % ny
    layers, hist, width = kbuf.shape
    parts = s1.shape[2]
    rows = tgt_ref.shape[0] // GROUPS
    head = width // HEADS
    factor = 0.5 / math.sqrt(head)
    wide = tile_of(width, 256)
    chunk = tile_of(hist, CHUNK)
    span = width // parts
    total_rows = nz * ny * rows
    bf, f32 = jnp.bfloat16, jnp.float32

    def at(zz, yy):
        return {"hist": zz * ny + yy}

    loads = []
    for l in range(layers):
        for k, (src, dst) in enumerate(
            ((wq_ref, wqb), (keys_ref, kbuf), (vals_ref, vbuf), (wg_ref, wgb), (wo_ref, wob))
        ):
            copy = pltpu.make_async_copy(src.at[l], dst.at[l], in_sem.at[l, k])
            copy.start()
            loads.append(copy)

    barrier = pltpu.get_barrier_semaphore()
    for j in range(1, nz):
        pl.semaphore_signal(barrier, inc=1, device_id=at((z + j) % nz, y), device_id_type=MESH)
    if ny == 2:
        pl.semaphore_signal(barrier, inc=1, device_id=at(z, 1 - y), device_id_type=MESH)
    hid[...] = tgt_ref[...].reshape(hid.shape)

    copies = {}

    def send(name, src, dst, ss, rs, dev):
        copy = pltpu.make_async_remote_copy(
            src_ref=src, dst_ref=dst, send_sem=ss, recv_sem=rs, device_id=dev, device_id_type=MESH
        )
        copy.start()
        copies[name] = copy

    def columns(i, size):
        return pl.ds(pl.multiple_of(i * size, size), size)

    def project(w_ref, g0, g1, store):
        def body(i, carry):
            cols = columns(i, wide)
            x = hid[g0:g1].reshape((g1 - g0) * rows, width)
            v = jnp.dot(x, w_ref[:, cols], preferred_element_type=f32)
            v = half_silu(v * 0.5)
            for g in range(g0, g1):
                store(g, cols, v[(g - g0) * rows : (g - g0 + 1) * rows])
            return carry

        lax.fori_loop(0, width // wide, body, 0, unroll=2)

    def query(l, g0, g1):
        def store(g, cols, v):
            q_all[l, g, z, y, :, cols] = v.astype(bf)

        project(wqb.at[l], g0, g1, store)

    def spread(l, g):
        mine = q_all.at[l, g, z, y]
        if ny == 2:
            send(("f", l, g, 0), mine, mine, fs_sem.at[l, g, 0], fr_sem.at[l, g, 0], at(z, 1 - y))
        for j in range(1, nz):
            send(
                ("z", l, g, j), mine, mine, zs_sem.at[l, g, j], zr_sem.at[l, g, j],
                at((z + j) % nz, y),
            )

    def gating(l, g0, g1):
        def store(g, cols, v):
            gate[g, :, cols] = v

        project(wgb.at[l], g0, g1, store)

    def forward(l, g):
        for j in range(1, nz):
            copies["z", l, g, j].wait_recv()
            if ny == 2:
                block = q_all.at[l, g, (z - j + nz) % nz, y]
                send(
                    ("f", l, g, j), block, block, fs_sem.at[l, g, j], fr_sem.at[l, g, j],
                    at(z, 1 - y),
                )

    def arrive(l, g):
        if ny == 2:
            for j in range(nz):
                copies["f", l, g, j].wait_recv()

    def attend(l, g, p):
        def body(i, carry):
            cols = columns(p * (HEADS // parts) + i, head)
            q = q_all[l, g, :, :, :, cols].reshape(total_rows, head)
            limit = lim_ref[g]
            total = jnp.zeros((total_rows, head), f32)
            for c in range(0, hist, chunk):
                s = lax.dot_general(
                    q, kbuf[l, c : c + chunk, cols], (((1,), (1,)), ((), ())),
                    preferred_element_type=f32,
                )
                w = half_silu((s * factor).astype(bf))
                pos = lax.broadcasted_iota(jnp.int32, s.shape, 1) + c
                w = jnp.where(pos < limit, w, jnp.bfloat16(0.0))
                total += jnp.dot(w, vbuf[l, c : c + chunk, cols], preferred_element_type=f32)
            res[g, :, :, :, cols] = total.reshape(nz, ny, rows, head)
            return carry

        lax.fori_loop(0, HEADS // parts, body, 0, unroll=UNROLL)
        if ny == 2:
            s1[l, g, p] = res[g, :, 1 - y, :, p * span : (p + 1) * span].astype(bf)
            send(
                ("1", l, g, p), s1.at[l, g, p], r1.at[l, g, p], s1_sem.at[l, g, p],
                r1_sem.at[l, g, p], at(z, 1 - y),
            )

    def reduce(l, g, p):
        if ny == 2:
            copies["1", l, g, p].wait_recv()
        for j in range(1, nz):
            zj = (z - j + nz) % nz
            term = res[g, zj, y, :, p * span : (p + 1) * span]
            if ny == 2:
                term = term + r1[l, g, p, zj].astype(f32)
            s2[l, g, p, j] = term.astype(bf)
            send(
                ("2", l, g, p, j), s2.at[l, g, p, j], r2.at[l, g, p, j], s2_sem.at[l, g, p, j],
                r2_sem.at[l, g, p, j], at(zj, y),
            )

    def finish(l, g):
        sums = []
        for p in range(parts):
            term = res[g, z, y, :, p * span : (p + 1) * span]
            if ny == 2:
                term = term + r1[l, g, p, z].astype(f32)
            for j in range(1, nz):
                copies["2", l, g, p, j].wait_recv()
                term = term + r2[l, g, p, j].astype(f32)
            sums.append(term)
        centre = sum(jnp.sum(t, axis=-1, keepdims=True) for t in sums) / width
        sums = [t - centre for t in sums]
        variance = sum(jnp.sum(jnp.square(t), axis=-1, keepdims=True) for t in sums) / width
        scale = lax.rsqrt(variance + 1e-05)
        for p, t in enumerate(sums):
            cols = slice(p * span, (p + 1) * span)
            normed[g, :, cols] = (t * scale * gain_ref[l : l + 1, cols] * gate[g, :, cols]).astype(bf)

        def body(i, carry):
            cols = columns(i, wide)
            update = jnp.dot(normed[g], wob[l, :, cols], preferred_element_type=f32)
            new = (hid[g, :, cols].astype(f32) + update).astype(bf)
            if l == layers - 1:
                out_ref[g * rows : (g + 1) * rows, cols] = new
            else:
                hid[g, :, cols] = new
            return carry

        lax.fori_loop(0, width // wide, body, 0, unroll=2)

    for l in range(layers):
        wait = loads[l * 5 : l * 5 + 5]
        if l == 0:
            wait[0].wait()
            query(0, 0, GROUPS)
            pl.semaphore_wait(barrier, nz - 1 + ny - 1)
            for g in range(GROUPS):
                spread(0, g)
            wait[3].wait()
            gating(0, 0, GROUPS)
        else:
            prev = GROUPS - 1
            wait[0].wait()
            for g in range(GROUPS):
                if g == prev:
                    reduce(l - 1, prev, parts - 1)
                    wait[3].wait()
                    if prev > 0:
                        gating(l, 0, prev)
                        forward(l, 0)
                finish(l - 1, g)
                query(l, g, g + 1)
                spread(l, g)
            gating(l, prev, GROUPS)
        wait[1].wait()
        wait[2].wait()
        wait[4].wait()
        if l == 0 or GROUPS == 1:
            forward(l, 0)
        arrive(l, 0)
        for g in range(GROUPS):
            for p in range(parts):
                attend(l, g, p)
                if p == 0 and g + 1 < GROUPS:
                    forward(l, g + 1)
                if p > 0:
                    reduce(l, g, p - 1)
                elif g > 0:
                    reduce(l, g - 1, parts - 1)
            if g + 1 < GROUPS:
                arrive(l, g + 1)
    last = layers - 1
    for g in range(GROUPS):
        if g == GROUPS - 1:
            reduce(last, g, parts - 1)
        finish(last, g)

    for copy in copies.values():
        copy.wait_send()


def inner_size(mesh):
    try:
        spot = mesh.axis_names.index("hist")
        line = mesh.devices.transpose(
            [spot] + [a for a in range(mesh.devices.ndim) if a != spot]
        ).reshape(mesh.devices.shape[spot], -1)[:, 0]
        ys = len({d.coords[1] for d in line})
    except (AttributeError, ValueError):
        ys = 1
    return ys if ys in (1, 2) and len(line) % ys == 0 else 1


def per_device(
    ny, targets, hist_keys, hist_values, lengths, cuts, w_query, w_gate, w_out, ln_gain
):
    layers, _, hist, width = hist_keys.shape
    rows = targets.shape[1]
    n = lax.axis_size("hist")
    nz = n // ny
    offset = lax.axis_index("hist") * hist
    rows //= GROUPS
    limits = jnp.minimum(cuts[0], lengths[0]) - offset
    limits = limits.reshape(n, GROUPS, rows).transpose(1, 0, 2).reshape(GROUPS, n * rows, 1)
    bf, f32 = jnp.bfloat16, jnp.float32
    vmem = pl.BlockSpec(memory_space=pltpu.VMEM)
    hbm = pl.BlockSpec(memory_space=pl.ANY)
    dma = pltpu.SemaphoreType.DMA
    span = width // PARTS
    refined = pl.pallas_call(
        functools.partial(kernel, ny, nz),
        out_shape=jax.ShapeDtypeStruct((GROUPS * rows, width), bf),
        in_specs=[vmem, vmem, hbm, hbm, hbm, hbm, hbm, vmem],
        out_specs=vmem,
        scratch_shapes=[
            pltpu.VMEM((layers, hist, width), bf),
            pltpu.VMEM((layers, hist, width), bf),
            pltpu.VMEM((layers, width, width), bf),
            pltpu.VMEM((layers, width, width), bf),
            pltpu.VMEM((layers, width, width), bf),
            pltpu.VMEM((layers, GROUPS, nz, ny, rows, width), bf),
            pltpu.VMEM((GROUPS, nz, ny, rows, width), f32),
            pltpu.VMEM((layers, GROUPS, PARTS, nz, rows, span), bf),
            pltpu.VMEM((layers, GROUPS, PARTS, nz, rows, span), bf),
            pltpu.VMEM((layers, GROUPS, PARTS, nz, rows, span), bf),
            pltpu.VMEM((layers, GROUPS, PARTS, nz, rows, span), bf),
            pltpu.VMEM((GROUPS, rows, width), f32),
            pltpu.VMEM((GROUPS, rows, width), bf),
            pltpu.VMEM((GROUPS, rows, width), bf),
            dma((layers, 5)),
        ]
        + [dma((layers, GROUPS, nz))] * 4
        + [dma((layers, GROUPS, PARTS))] * 2
        + [dma((layers, GROUPS, PARTS, nz))] * 2,
        compiler_params=pltpu.CompilerParams(
            collective_id=0, has_side_effects=True, vmem_limit_bytes=60 * 2**20
        ),
    )(
        limits, targets[0], hist_keys[:, 0], hist_values[:, 0], w_query, w_gate, w_out, ln_gain
    )
    return refined[None]


def solution(mesh):
    return jax.shard_map(
        functools.partial(per_device, inner_size(mesh)),
        mesh=mesh,
        in_specs=(
            P(("groups", "users"), "hist", None),
            P(None, ("groups", "users"), "hist", None),
            P(None, ("groups", "users"), "hist", None),
            P(("groups", "users")),
            P(("groups", "users"), None),
            P(),
            P(),
            P(),
            P(),
        ),
        out_specs=P(("groups", "users"), "hist", None),
        check_vma=False,
    )
```
